512 devices in a mesh: tm: 64 (over y, z), head: 8 (over x, core).
Axes of the slice: x: 4, y: 8, z: 8, core: 2. Of those that a mesh axis runs over, the one named last changes fastest.
Arguments:
- queries: bfloat16 [16384, 3072], P('tm', 'head'), may hold values from -6 to 6
- keys: bfloat16 [8192, 3072], P('tm', 'head'), may hold values from -6 to 6
- values: bfloat16 [8192, 3072], P('tm', 'head'), may hold values from -6 to 6
- out_weight: bfloat16 [3072, 3072], P('head'), may hold values from -0.109375 to 0.109375
- out_grad: bfloat16 [16384, 3072], P('tm', 'head'), may hold values from -6 to 6
- align_lists: int32 [64, 4], replicated, may hold values from -1 to 63, as said below
- block_masks: int32 [128, 3], P('tm'), may hold values from -1 to 3, as said below
Outputs:
- mixed: bfloat16 [16384, 3072], P('tm', 'head')
- query_grad: bfloat16 [16384, 3072], P('tm', 'head')
- key_grad: bfloat16 [8192, 3072], P('tm', 'head')
- value_grad: bfloat16 [8192, 3072], P('tm', 'head')
The draws below stay inside these ranges and needn't reach their ends.
Inputs may be any that keep to these rules, and one draw needn't show every extreme that they name: `align_lists`: row t holds a band of consecutive audio tile indices in its first slots and -1 in the rest; every listed tile a satisfies (t - 3) <= a < (t + 4). Some slab uses all 4 slots starting at (t - 3), and some slab's band ends at (t + 4) - 1. `block_masks`: row i names one or more consecutive used slots of the list of slab i // 2 in its first entries and -1 in the rest; some row has all 3 entries live.
All inputs are finite; a program needn't handle non-finite values.
Results may differ from the reference program's by a relative error of at most 0.025.
Values may be sent and summed in bfloat16 or wider, within the bound.
No kernel may reach another device: no remote copies, remote signals or barrier semaphores. Data moves between devices by JAX's collectives and lax.ppermute only.
A program may use at most 64 MiB of HBM per device.

```python
import math
import jax
import jax.numpy as jnp
from jax import lax

D = 3072
HEADS = 24
HEAD_DIM = 128
TILE = 128
VT_DEV = 2
AB_DEV = 1
LIST = 4
BLOCKS = 3
REACH = 3
SLABS = 64
INNER = 3072
VTILES = 128
ATILES = 64
VIDEO = 16384
AUDIO = 8192
N_HEAD = 8


def draw_layout(key):
    base_key = jax.random.fold_in(key, 11)
    k_len, k_start, k_pick, k_count, k_shift = jax.random.split(base_key, 5)
    slab_index = jnp.arange(SLABS)
    region_lo = jnp.maximum(0, (slab_index - REACH) * AB_DEV)
    region_hi = jnp.minimum(ATILES, (slab_index + REACH + 1) * AB_DEV)
    band_len = jax.random.randint(k_len, (SLABS,), 1, LIST + 1)
    inner_span = SLABS - 2 * REACH
    full_slab = REACH + jax.random.randint(k_pick, (), 0, inner_span)
    edge_slab = REACH + (full_slab - REACH + 1) % inner_span
    band_len = jnp.where((slab_index == full_slab) | (slab_index == edge_slab), LIST, band_len)
    free_room = region_hi - region_lo - band_len + 1
    band_start = region_lo + jax.random.randint(k_start, (SLABS,), 0, 1 << 20) % free_room
    band_start = jnp.where(slab_index == full_slab, region_lo, band_start)
    band_start = jnp.where(slab_index == edge_slab, region_hi - band_len, band_start)
    slot_index = jnp.arange(LIST)
    align_table = jnp.where(slot_index[None, :] < band_len[:, None], band_start[:, None] + slot_index[None, :], -1)
    tile_slab = jnp.arange(VTILES) // VT_DEV
    tile_band = band_len[tile_slab]
    most_live = jnp.minimum(BLOCKS, tile_band)
    live_count = 1 + jax.random.randint(k_count, (VTILES,), 0, 1 << 20) % most_live
    live_count = jnp.where(jnp.arange(VTILES) == full_slab * VT_DEV, BLOCKS, live_count)
    live_offset = jax.random.randint(k_shift, (VTILES,), 0, 1 << 20) % (tile_band - live_count + 1)
    place_index = jnp.arange(BLOCKS)
    block_table = jnp.where(place_index[None, :] < live_count[:, None], live_offset[:, None] + place_index[None, :], -1)
    return (align_table.astype(jnp.int32), block_table.astype(jnp.int32))


def audio_keys(key):
    raw_keys = jax.random.normal(jax.random.fold_in(key, 23), (AUDIO, HEADS * HEAD_DIM), jnp.float32)
    raw_keys = jnp.clip(raw_keys, -6.0, 6.0)
    return raw_keys


def draw_align_lists(key, part):
    return draw_layout(key)[0]


def draw_block_masks(key, part):
    return draw_layout(key)[1]


def draw_keys(key, part):
    return audio_keys(key).astype(jnp.bfloat16)


def draw_queries(key, part):
    drawn_rows = jax.random.normal(jax.random.fold_in(key, 31), (VIDEO, HEADS * HEAD_DIM), jnp.float32)
    drawn_rows = jnp.clip(drawn_rows, -6.0, 6.0)
    return drawn_rows.astype(jnp.bfloat16)


def block_levels(stream_key, dims, cuts, least, high):
    gain = 1.0
    for dim, parts in cuts:
        heights = jax.random.uniform(jax.random.fold_in(jax.random.fold_in(stream_key, 6), dim), (parts,), jnp.float32, least / len(cuts), high / len(cuts))
        gain = gain * jnp.repeat(jnp.exp(heights), dims[dim] // parts).reshape((-1,) + (1,) * (len(dims) - 1 - dim))
    return gain


def scatter_about(stream_key, dims, deviation, most, cuts=(), kind=jnp.bfloat16):
    entries = deviation * jax.random.normal(stream_key, dims, jnp.float32)
    if cuts:
        entries = entries * block_levels(stream_key, dims, cuts, -0.22, 0.18)
    return jnp.clip(entries, -most, most).astype(kind)


def setup_inputs(seed: int = 0) -> dict:
    arg_keys = jax.random.split(jax.random.key(seed), 8)
    queries = draw_queries(jax.random.fold_in(arg_keys[7], 71), 0)
    keys = draw_keys(jax.random.fold_in(arg_keys[7], 71), 0)
    values = scatter_about(arg_keys[2], (AUDIO, INNER), 1.0, 6.0, ((0, 64), (1, 8)))
    out_weight = scatter_about(arg_keys[3], (INNER, D), INNER ** -0.5, 0.109375, ((0, 8),))
    out_grad = scatter_about(arg_keys[4], (VIDEO, D), 1.0, 6.0, ((0, 64), (1, 8)))
    align_lists = draw_align_lists(jax.random.fold_in(arg_keys[7], 71), 0)
    block_masks = draw_block_masks(jax.random.fold_in(arg_keys[7], 71), 0)
    return {"queries": queries, "keys": keys, "values": values, "out_weight": out_weight, "out_grad": out_grad, "align_lists": align_lists, "block_masks": block_masks}


def round_keep(value):
    return lax.optimization_barrier(value.astype(jnp.bfloat16)).astype(jnp.float32)

def tile_probs(query_tile, key_rows, live_tile):
    score_scale = 1.0 / math.sqrt(HEAD_DIM)
    query_heads = query_tile.astype(jnp.float32).reshape(TILE, HEADS, HEAD_DIM)
    key_heads = key_rows.astype(jnp.float32).reshape(BLOCKS * TILE, HEADS, HEAD_DIM)
    scores = jnp.einsum('qhd,khd->hqk', query_heads, key_heads) * score_scale
    key_live = jnp.repeat(live_tile, TILE)
    scores = jnp.where(key_live[None, None, :], scores, -jnp.inf)
    row_top = lax.optimization_barrier(jnp.max(scores, -1, keepdims=True))
    exp_scores = jnp.exp(scores - row_top)
    return exp_scores / lax.optimization_barrier(jnp.sum(exp_scores, -1, keepdims=True))

def reference(queries, keys, values, out_weight, out_grad, align_lists, block_masks):
    inner = HEADS * HEAD_DIM
    score_scale = 1.0 / math.sqrt(HEAD_DIM)
    tile_slab = jnp.arange(VTILES, dtype=jnp.int32) // VT_DEV
    live_block = block_masks >= 0
    picked = jnp.take_along_axis(align_lists[tile_slab], jnp.maximum(block_masks, 0), axis=1)
    picked = jnp.where(live_block, picked, 0).astype(jnp.int32)
    key_tiles = keys.reshape(ATILES, TILE, inner)
    value_tiles = values.reshape(ATILES, TILE, inner)
    query_tiles = queries.reshape(VTILES, TILE, inner)

    def forward_tile(operands):
        query_tile, picked_tile, live_tile = operands
        soft_probs = tile_probs(query_tile, key_tiles[picked_tile], live_tile)
        weights = round_keep(soft_probs)
        value_heads = value_tiles[picked_tile].astype(jnp.float32).reshape(BLOCKS * TILE, HEADS, HEAD_DIM)
        return jnp.einsum('hqk,khd->qhd', weights, value_heads).astype(jnp.bfloat16).reshape(TILE, inner)
    attended = lax.map(forward_tile, (query_tiles, picked, live_block)).reshape(VIDEO, inner)
    group_cols = inner // N_HEAD
    mixed_sum = jnp.zeros((VIDEO, D), jnp.float32)
    for group_index in range(N_HEAD):
        low = group_index * group_cols
        partial_sum = jnp.dot(attended[:, low:low + group_cols], out_weight[low:low + group_cols], preferred_element_type=jnp.float32)
        mixed_sum = mixed_sum + round_keep(partial_sum)
    mixed = mixed_sum.astype(jnp.bfloat16)
    grad_attended = jnp.dot(out_grad, out_weight.T, preferred_element_type=jnp.float32).astype(jnp.bfloat16)
    grad_tiles = grad_attended.reshape(VTILES, TILE, inner)
    attended_tiles = attended.reshape(VTILES, TILE, inner)

    def backward_tile(sums_carry, operands):
        key_sum, value_sum = sums_carry
        query_tile, grad_tile, attended_tile, picked_tile, live_tile = operands
        key_rows = key_tiles[picked_tile]
        value_rows = value_tiles[picked_tile]
        soft_probs = tile_probs(query_tile, key_rows, live_tile)
        weights = round_keep(soft_probs)
        query_heads = query_tile.astype(jnp.float32).reshape(TILE, HEADS, HEAD_DIM)
        key_heads = key_rows.astype(jnp.float32).reshape(BLOCKS * TILE, HEADS, HEAD_DIM)
        value_heads = value_rows.astype(jnp.float32).reshape(BLOCKS * TILE, HEADS, HEAD_DIM)
        grad_heads = grad_tile.astype(jnp.float32).reshape(TILE, HEADS, HEAD_DIM)
        attended_heads = attended_tile.astype(jnp.float32).reshape(TILE, HEADS, HEAD_DIM)
        row_delta = lax.optimization_barrier(jnp.sum(grad_heads * attended_heads, -1))
        grad_probs = jnp.einsum('qhd,khd->hqk', grad_heads, value_heads)
        grad_scores = round_keep(soft_probs * (grad_probs - row_delta.T[:, :, None]))
        query_grad = (jnp.einsum('hqk,khd->qhd', grad_scores, key_heads) * score_scale).astype(jnp.bfloat16).reshape(TILE, inner)
        key_terms = (jnp.einsum('hqk,qhd->khd', grad_scores, query_heads) * score_scale).reshape(BLOCKS, TILE, inner)
        value_terms = jnp.einsum('hqk,qhd->khd', weights, grad_heads).reshape(BLOCKS, TILE, inner)
        keep_block = live_tile[:, None, None]
        key_sum = key_sum.at[picked_tile].add(jnp.where(keep_block, key_terms, jnp.zeros_like(key_terms)))
        value_sum = value_sum.at[picked_tile].add(jnp.where(keep_block, value_terms, jnp.zeros_like(value_terms)))
        return ((key_sum, value_sum), query_grad)
    zero_sum = jnp.zeros((ATILES, TILE, inner), jnp.float32)
    (key_sum, value_sum), query_grad = lax.scan(backward_tile, (zero_sum, zero_sum), (query_tiles, grad_tiles, attended_tiles, picked, live_block))
    key_grad = key_sum.reshape(AUDIO, inner).astype(jnp.bfloat16)
    value_grad = value_sum.reshape(AUDIO, inner).astype(jnp.bfloat16)
    return (mixed, query_grad.reshape(VIDEO, inner), key_grad, value_grad)
```

```python
import functools
import math

import jax
import jax.numpy as jnp
from jax import lax
from jax.experimental import pallas as pl
from jax.experimental.pallas import tpu as pltpu
from jax.sharding import PartitionSpec as P

HEAD_DIM = 128
TILE = 128
BLOCKS = 3
LIST = 4
REACH = 3
SPAN = 2 * REACH + 1

VMEM = pltpu.VMEM
SMEM = pltpu.SMEM


def nt(a, b):
    return lax.dot_general(a, b, (((1,), (1,)), ((), ())), preferred_element_type=jnp.float32)


def tn(a, b):
    return lax.dot_general(a, b, (((0,), (0,)), ((), ())), preferred_element_type=jnp.float32)


def nn(a, b):
    return lax.dot_general(a, b, (((1,), (0,)), ((), ())), preferred_element_type=jnp.float32)


def grad_attended_kernel(where_ref, mine_ref, theirs_ref, weight_ref, out_ref):
    rows, cols = out_ref.shape
    total = None
    for n, ref in enumerate((mine_ref, theirs_ref)):
        for b in range(4):
            low = pl.multiple_of(where_ref[n * 4 + b] * cols, 128)
            term = nt(ref[pl.ds(b * rows, rows), :], weight_ref[:, pl.ds(low, cols)])
            total = term if total is None else total + term
    out_ref[...] = total.astype(out_ref.dtype)


def out_proj_kernel(where_ref, attended_ref, weight_ref, send_ref, keep_ref):
    rows, cols = attended_ref.shape
    attended = attended_ref[...]
    for n, ref in enumerate((send_ref, keep_ref)):
        for b in range(4):
            low = pl.multiple_of(where_ref[n * 4 + b] * cols, 128)
            ref[pl.ds(b * rows, rows), :] = nn(attended, weight_ref[:, pl.ds(low, cols)]).astype(ref.dtype)


def attention_kernel(slab_ref, align_ref, mask_ref, query_ref, grad_ref, *refs):
    tile_refs = refs[:SPAN]
    attended_ref, query_grad_ref = refs[SPAN : SPAN + 2]
    term_refs = refs[SPAN + 2 : 2 * SPAN + 2]
    region, sums = refs[2 * SPAN + 2 :]
    cols = query_ref.shape[1]
    heads = cols // HEAD_DIM
    tiles = query_ref.shape[0] // TILE
    score_scale = 1.0 / math.sqrt(HEAD_DIM)
    slab = slab_ref[0]
    for n in range(SPAN):
        region[pl.ds(n * 2 * TILE, 2 * TILE), :] = tile_refs[n][...]
    sums[...] = jnp.zeros_like(sums)
    for i in range(tiles):
        key_lows, live = [], []
        for b in range(BLOCKS):
            slot = mask_ref[i, b]
            picked = align_ref[slab, jnp.clip(slot, 0, LIST - 1)]
            local = jnp.clip(picked - slab + REACH, 0, SPAN - 1)
            live.append(slot >= 0)
            key_lows.append(pl.multiple_of(jnp.where(slot >= 0, local, 0) * (2 * TILE), 2 * TILE))
        for h in range(heads):
            rows, hcols = pl.ds(i * TILE, TILE), pl.ds(h * HEAD_DIM, HEAD_DIM)
            query = query_ref[rows, hcols]
            grad = grad_ref[rows, hcols]
            keys = [region[pl.ds(low, TILE), hcols] for low in key_lows]
            values = [region[pl.ds(low + TILE, TILE), hcols] for low in key_lows]
            scores = [
                jnp.where(live[b], nt(query, keys[b]) * score_scale, -jnp.inf) for b in range(BLOCKS)
            ]
            top = jnp.max(jnp.maximum(jnp.maximum(scores[0], scores[1]), scores[2]), -1, keepdims=True)
            exps = [jnp.exp(s - top) for s in scores]
            norm = jnp.sum(exps[0] + exps[1] + exps[2], -1, keepdims=True)
            probs = [e / norm for e in exps]
            weights = [p.astype(jnp.bfloat16) for p in probs]
            attended = nn(weights[0], values[0]) + nn(weights[1], values[1]) + nn(weights[2], values[2])
            attended = attended.astype(jnp.bfloat16)
            attended_ref[rows, hcols] = attended
            delta = jnp.sum(grad.astype(jnp.float32) * attended.astype(jnp.float32), -1, keepdims=True)
            grad_scores = [
                (probs[b] * (nt(grad, values[b]) - delta)).astype(jnp.bfloat16) for b in range(BLOCKS)
            ]
            query_grad = (
                nn(grad_scores[0], keys[0]) + nn(grad_scores[1], keys[1]) + nn(grad_scores[2], keys[2])
            )
            query_grad_ref[rows, hcols] = (query_grad * score_scale).astype(query_grad_ref.dtype)
            for b in range(BLOCKS):
                at_key, at_value = pl.ds(key_lows[b], TILE), pl.ds(key_lows[b] + TILE, TILE)
                sums[at_key, hcols] += tn(grad_scores[b], query) * score_scale
                sums[at_value, hcols] += tn(weights[b], grad)
    for n in range(SPAN):
        term_refs[n][...] = sums[pl.ds(n * 2 * TILE, 2 * TILE), :].astype(term_refs[n].dtype)


def vm():
    return pl.BlockSpec(memory_space=VMEM)


def sm():
    return pl.BlockSpec(memory_space=SMEM)


def local(queries, keys, values, out_weight, out_grad, align_lists, block_masks):
    slabs = lax.axis_size("tm")
    groups = lax.axis_size("head")
    chips = groups // 2
    slab = lax.axis_index("tm")
    group = lax.axis_index("head")
    chip, core = group // 2, group % 2
    rows, cols = queries.shape
    bf16, f32 = jnp.bfloat16, jnp.float32

    def along(x, by):
        return lax.ppermute(x, "tm", [(t, (t + by) % slabs) for t in range(slabs)])

    def across(x, by0, by1):
        pairs = [
            (2 * c + k, 2 * ((c + (by1 if k else by0)) % chips) + k)
            for c in range(chips)
            for k in range(2)
        ]
        return lax.ppermute(x, "head", pairs)

    def swap(x):
        return lax.ppermute(x, "head", [(g, g ^ 1) for g in range(groups)])

    own = jnp.concatenate([keys, values], 0)
    right, left = [], []
    r = l = own
    gathered = [out_grad]
    for n in range(REACH):
        r = along(r, 1)
        right.append(r)
        if n == 0:
            a_block = across(out_grad, 1, -1)
        l = along(l, -1)
        left.append(l)
        if n == 0:
            b_block = across(out_grad, -1, 1)
        if n == 1:
            c_block = across(a_block, 1, -1)
    mine = jnp.concatenate([out_grad, a_block, b_block, c_block], 0)
    theirs = swap(mine)

    def block_of(k, step):
        return 2 * ((chip + step) % chips) + k

    def order(k):
        step = jnp.where(k == 0, -1, 1)
        return [block_of(k, 0), block_of(k, step), block_of(k, -step), block_of(k, 2)]

    gather_order = jnp.stack(order(core) + order(1 - core)).astype(jnp.int32)
    scatter_order = jnp.stack(
        [block_of(1 - core, s) for s in range(4)] + [block_of(core, s) for s in range(4)]
    ).astype(jnp.int32)
    slab_array = jnp.full((1,), slab, jnp.int32)

    grad_attended = pl.pallas_call(
        grad_attended_kernel,
        out_shape=jax.ShapeDtypeStruct((rows, cols), bf16),
        in_specs=[sm(), vm(), vm(), vm()],
        out_specs=vm(),
        cost_estimate=pl.CostEstimate(
            flops=2 * rows * cols * 8 * cols, bytes_accessed=8 * cols * (rows + cols) * 2, transcendentals=0
        ),
        name="grad_attended",
    )(gather_order, mine, theirs, out_weight)

    tile_shape = jax.ShapeDtypeStruct((2 * TILE, cols), bf16)
    outs = pl.pallas_call(
        attention_kernel,
        out_shape=[jax.ShapeDtypeStruct((rows, cols), bf16)] * 2
        + [tile_shape] * REACH
        + [jax.ShapeDtypeStruct((2 * TILE, cols), f32)]
        + [tile_shape] * REACH,
        in_specs=[sm(), sm(), sm()] + [vm()] * (2 + SPAN),
        out_specs=[vm()] * (2 + SPAN),
        scratch_shapes=[VMEM((SPAN * 2 * TILE, cols), bf16), VMEM((SPAN * 2 * TILE, cols), f32)],
        cost_estimate=pl.CostEstimate(
            flops=14 * rows * cols * BLOCKS * TILE, bytes_accessed=20 * rows * cols * 2, transcendentals=rows * 1152
        ),
        name="attention",
    )(
        slab_array, align_lists, block_masks, queries, grad_attended,
        right[2], right[1], right[0], own, left[0], left[1], left[2],
    )
    attended, query_grad = outs[:2]
    terms = outs[2:]

    send, keep = pl.pallas_call(
        out_proj_kernel,
        out_shape=[jax.ShapeDtypeStruct((4 * rows, cols), bf16)] * 2,
        in_specs=[sm(), vm(), vm()],
        out_specs=[vm(), vm()],
        cost_estimate=pl.CostEstimate(
            flops=2 * rows * cols * 8 * cols, bytes_accessed=8 * cols * (rows + cols) * 2, transcendentals=0
        ),
        name="out_proj",
    )(scatter_order, attended, out_weight)

    def add(x, y):
        return (x.astype(f32) + y.astype(f32)).astype(bf16)

    rightward, leftward = terms[2 * REACH], terms[0]
    arrived = None
    for n in range(REACH - 1, -1, -1):
        rightward = along(rightward, 1)
        leftward = along(leftward, -1)
        if n:
            rightward = add(rightward, terms[REACH + n])
            leftward = add(leftward, terms[REACH - n])
        if n == REACH - 1:
            pair_sums = add(keep, swap(send)).reshape(4, rows, cols)
            arrived = [across(pair_sums[s], s, s) for s in (1, 3, 2)]
    total = terms[REACH] + rightward.astype(f32) + leftward.astype(f32)
    key_grad = total[:TILE].astype(bf16)
    value_grad = total[TILE:].astype(bf16)
    mixed = pair_sums[0].astype(f32)
    for part in arrived:
        mixed = mixed + part.astype(f32)
    return (mixed.astype(bf16), query_grad, key_grad, value_grad)


def solution(mesh):
    return jax.shard_map(
        local,
        mesh=mesh,
        in_specs=(
            P("tm", "head"),
            P("tm", "head"),
            P("tm", "head"),
            P("head", None),
            P("tm", "head"),
            P(),
            P("tm", None),
        ),
        out_specs=(P("tm", "head"), P("tm", "head"), P("tm", "head"), P("tm", "head")),
        check_vma=False,
    )
```

```python
import functools
import math

import jax
import jax.numpy as jnp
from jax import lax
from jax.experimental import pallas as pl
from jax.experimental.pallas import tpu as pltpu
from jax.sharding import PartitionSpec as P


HEAD_DIM = 128
TILE = 128
BLOCKS = 3
LIST = 4
REACH = 3
SPAN = 2 * REACH + 1
LIMIT = 24 * 1024 * 1024

VMEM = pltpu.VMEM
SMEM = pltpu.SMEM


def nt(a, b):
    return lax.dot_general(a, b, (((1,), (1,)), ((), ())), preferred_element_type=jnp.float32)


def tn(a, b):
    return lax.dot_general(a, b, (((0,), (0,)), ((), ())), preferred_element_type=jnp.float32)


def nn(a, b):
    return lax.dot_general(a, b, (((1,), (0,)), ((), ())), preferred_element_type=jnp.float32)


def block_of(group, flip, step, chips):
    return (((group >> 1) + step) & (chips - 1)) * 2 + ((group & 1) ^ flip)


def grad_attended_kernel(chips, group_ref, mine_ref, theirs_ref, weight_ref, out_ref):
    rows, cols = out_ref.shape
    group = group_ref[0]
    total = None
    for flip, ref in enumerate((mine_ref, theirs_ref)):
        step = (((group & 1) ^ flip) << 1) - 1
        for b, by in enumerate((0, step, -step, 2)):
            low = pl.multiple_of(block_of(group, flip, by, chips) * cols, 128)
            term = nt(ref[pl.ds(b * rows, rows), :], weight_ref[:, pl.ds(low, cols)])
            total = term if total is None else total + term
    out_ref[...] = total.astype(out_ref.dtype)


def out_proj_kernel(chips, group_ref, attended_ref, weight_ref, send_ref, keep_ref):
    rows, cols = attended_ref.shape
    group = group_ref[0]
    attended = attended_ref[...]
    for flip, ref in ((1, send_ref), (0, keep_ref)):
        for b in range(4):
            low = pl.multiple_of(block_of(group, flip, b, chips) * cols, 128)
            ref[pl.ds(b * rows, rows), :] = nn(attended, weight_ref[:, pl.ds(low, cols)]).astype(ref.dtype)


def attention_kernel(slab_ref, align_ref, mask_ref, query_ref, grad_ref, *refs):
    tile_refs = refs[:SPAN]
    attended_ref, query_grad_ref = refs[SPAN : SPAN + 2]
    term_refs = refs[SPAN + 2 : 2 * SPAN + 2]
    region, sums = refs[2 * SPAN + 2 :]
    cols = query_ref.shape[1]
    heads = cols // HEAD_DIM
    tiles = query_ref.shape[0] // TILE
    score_scale = 1.0 / math.sqrt(HEAD_DIM)
    slab = slab_ref[0]
    for n in range(SPAN):
        region[pl.ds(n * 2 * TILE, 2 * TILE), :] = tile_refs[n][...]
    sums[...] = jnp.zeros_like(sums)
    for i in range(tiles):
        key_lows, live = [], []
        for b in range(BLOCKS):
            slot = mask_ref[i, b]
            picked = align_ref[jnp.clip(slot, 0, LIST - 1), slab]
            local = jnp.clip(picked - slab + REACH, 0, SPAN - 1)
            live.append(slot >= 0)
            key_lows.append(pl.multiple_of(jnp.where(slot >= 0, local, 0) * (2 * TILE), 2 * TILE))
        for h in range(heads):
            rows, hcols = pl.ds(i * TILE, TILE), pl.ds(h * HEAD_DIM, HEAD_DIM)
            query = query_ref[rows, hcols]
            grad = grad_ref[rows, hcols]
            keys = [region[pl.ds(low, TILE), hcols] for low in key_lows]
            values = [region[pl.ds(low + TILE, TILE), hcols] for low in key_lows]
            scores = [
                jnp.where(live[b], nt(query, keys[b]) * score_scale, -jnp.inf) for b in range(BLOCKS)
            ]
            top = jnp.max(jnp.maximum(jnp.maximum(scores[0], scores[1]), scores[2]), -1, keepdims=True)
            exps = [jnp.exp(s - top) for s in scores]
            norm = jnp.sum(exps[0] + exps[1] + exps[2], -1, keepdims=True)
            inverse = 1.0 / norm
            probs = [e * inverse for e in exps]
            weights = [p.astype(jnp.bfloat16) for p in probs]
            attended = nn(weights[0], values[0]) + nn(weights[1], values[1]) + nn(weights[2], values[2])
            attended = attended.astype(jnp.bfloat16)
            attended_ref[rows, hcols] = attended
            delta = jnp.sum(grad.astype(jnp.float32) * attended.astype(jnp.float32), -1, keepdims=True)
            grad_scores = [
                (probs[b] * (nt(grad, values[b]) - delta)).astype(jnp.bfloat16) for b in range(BLOCKS)
            ]
            query_grad = (
                nn(grad_scores[0], keys[0]) + nn(grad_scores[1], keys[1]) + nn(grad_scores[2], keys[2])
            )
            query_grad_ref[rows, hcols] = (query_grad * score_scale).astype(query_grad_ref.dtype)
            for b in range(BLOCKS):
                at_key, at_value = pl.ds(key_lows[b], TILE), pl.ds(key_lows[b] + TILE, TILE)
                sums[at_key, hcols] += tn(grad_scores[b], query) * score_scale
                sums[at_value, hcols] += tn(weights[b], grad)
    for n in range(SPAN):
        term_refs[n][...] = sums[pl.ds(n * 2 * TILE, 2 * TILE), :].astype(term_refs[n].dtype)


def vm():
    return pl.BlockSpec(memory_space=VMEM)


def sm():
    return pl.BlockSpec(memory_space=SMEM)


def step(queries, keys, values, out_weight, out_grad, align_lists, block_masks):
    slabs = lax.axis_size("tm")
    groups = lax.axis_size("head")
    chips = groups // 2
    slab = jnp.full((1,), lax.axis_index("tm"), jnp.int32)
    group = jnp.full((1,), lax.axis_index("head"), jnp.int32)
    rows, cols = queries.shape
    bf16, f32 = jnp.bfloat16, jnp.float32

    def along(x, by):
        return lax.ppermute(x, "tm", [(t, (t + by) % slabs) for t in range(slabs)])

    def across(x, by0, by1):
        pairs = [
            (2 * c + k, 2 * ((c + (by1 if k else by0)) % chips) + k)
            for c in range(chips)
            for k in range(2)
        ]
        return lax.ppermute(x, "head", pairs)

    def swap(x):
        return lax.ppermute(x, "head", [(g, g ^ 1) for g in range(groups)])

    def kernel(body, args, in_specs, outs, scratch=(), flops=0, limit=None, exps=0):
        moved = sum(math.prod(a.shape) * a.dtype.itemsize for a in (*args, *outs))
        return pl.pallas_call(
            body,
            out_shape=outs,
            in_specs=in_specs,
            out_specs=[vm()] * len(outs),
            scratch_shapes=list(scratch),
            compiler_params=pltpu.CompilerParams(vmem_limit_bytes=limit),
            cost_estimate=pl.CostEstimate(flops=flops, bytes_accessed=moved, transcendentals=exps),
        )(*args)

    block = jax.ShapeDtypeStruct((rows, cols), bf16)
    own = jnp.concatenate([keys, values], 0)
    a_block = across(out_grad, 1, -1)
    r1 = along(own, 1)
    b_block = across(out_grad, -1, 1)
    l1 = along(own, -1)
    c_block = across(a_block, 1, -1)
    r2 = along(r1, 1)
    l2 = along(l1, -1)
    mine = jnp.concatenate([out_grad, a_block, b_block, c_block], 0)
    theirs = swap(mine)
    r3 = along(r2, 1)
    l3 = along(l2, -1)

    (grad_attended,) = kernel(
        functools.partial(grad_attended_kernel, chips),
        (group, mine, theirs, out_weight),
        [sm(), vm(), vm(), vm()],
        [block],
        flops=2 * rows * cols * groups * cols,
        limit=LIMIT,
    )
    outs = kernel(
        attention_kernel,
        (slab, align_lists.T, block_masks, queries, grad_attended, r3, r2, r1, own, l1, l2, l3),
        [sm()] * 3 + [vm()] * (2 + SPAN),
        [block] * (2 + REACH) + [jax.ShapeDtypeStruct(own.shape, f32)] + [block] * REACH,
        scratch=(VMEM((SPAN * 2 * TILE, cols), bf16), VMEM((SPAN * 2 * TILE, cols), f32)),
        flops=14 * rows * cols * BLOCKS * TILE,
        exps=rows * cols * BLOCKS,
        limit=LIMIT,
    )
    attended, query_grad = outs[:2]
    terms = outs[2:]
    send, keep = kernel(
        functools.partial(out_proj_kernel, chips),
        (group, attended, out_weight),
        [sm(), vm(), vm()],
        [jax.ShapeDtypeStruct((4 * rows, cols), bf16)] * 2,
        flops=2 * rows * cols * groups * cols,
        limit=LIMIT,
    )

    def add(x, y):
        return (x.astype(f32) + y.astype(f32)).astype(bf16)

    rightward, leftward = terms[2 * REACH], terms[0]
    for n in range(REACH, 0, -1):
        rightward = along(rightward, 1)
        leftward = along(leftward, -1)
        if n > 1:
            rightward = add(rightward, terms[REACH + n - 1])
            leftward = add(leftward, terms[REACH - n + 1])
    pair_sums = add(keep, swap(send)).reshape(4, rows, cols)
    arrived = [across(pair_sums[s], s, s) for s in (1, 3, 2)]
    total = terms[REACH] + rightward.astype(f32) + leftward.astype(f32)
    key_grad = total[:TILE].astype(bf16)
    value_grad = total[TILE:].astype(bf16)
    mixed = pair_sums[0].astype(f32)
    for part in arrived:
        mixed = mixed + part.astype(f32)
    return (mixed.astype(bf16), query_grad, key_grad, value_grad)


def solution(mesh):
    return jax.shard_map(
        step,
        mesh=mesh,
        in_specs=(
            P("tm", "head"),
            P("tm", "head"),
            P("tm", "head"),
            P("head", None),
            P("tm", "head"),
            P(),
            P("tm", None),
        ),
        out_specs=(P("tm", "head"), P("tm", "head"), P("tm", "head"), P("tm", "head")),
        check_vma=False,
    )
```

```python
import math

import jax
import jax.numpy as jnp
from jax import lax
from jax.experimental import pallas as pl
from jax.experimental.pallas import tpu as pltpu
from jax.sharding import PartitionSpec as P


HEAD_DIM = 128
TILE = 128
BLOCKS = 3
LIST = 4
REACH = 3
SPAN = 2 * REACH + 1
HOPS = (0, 1, 3, 2)
LIMIT = 24 * 1024 * 1024

VMEM = pltpu.VMEM
SMEM = pltpu.SMEM


def nt(a, b):
    return lax.dot_general(a, b, (((1,), (1,)), ((), ())), preferred_element_type=jnp.float32)


def tn(a, b):
    return lax.dot_general(a, b, (((0,), (0,)), ((), ())), preferred_element_type=jnp.float32)


def nn(a, b):
    return lax.dot_general(a, b, (((1,), (0,)), ((), ())), preferred_element_type=jnp.float32)


def block_of(group, flip, hop):
    return ((group >> 1) ^ hop) * 2 + ((group & 1) ^ flip)


def grad_attended_kernel(group_ref, mine_ref, theirs_ref, weight_ref, out_ref):
    rows, cols = out_ref.shape
    group = group_ref[0]
    total = None
    for flip, ref in enumerate((mine_ref, theirs_ref)):
        for b, hop in enumerate(HOPS):
            low = pl.multiple_of(block_of(group, flip, hop) * cols, 128)
            term = nt(ref[pl.ds(b * rows, rows), :], weight_ref[:, pl.ds(low, cols)])
            total = term if total is None else total + term
    out_ref[...] = total.astype(out_ref.dtype)


def out_proj_kernel(group_ref, attended_ref, weight_ref, send_ref, *keep_refs):
    rows, cols = attended_ref.shape
    group = group_ref[0]
    attended = attended_ref[...]
    for b, hop in enumerate(HOPS):
        low = pl.multiple_of(block_of(group, 1, hop) * cols, 128)
        send_ref[pl.ds(b * rows, rows), :] = nn(attended, weight_ref[:, pl.ds(low, cols)]).astype(send_ref.dtype)
    for b, hop in enumerate(HOPS):
        low = pl.multiple_of(block_of(group, 0, hop) * cols, 128)
        product = nn(attended, weight_ref[:, pl.ds(low, cols)])
        ref = keep_refs[b // 2]
        ref[pl.ds(b % 2 * rows, rows), :] = product.astype(ref.dtype)


def attention_kernel(slab_ref, group_ref, align_ref, mask_ref, query_ref, grad_ref, *refs):
    tile_refs = refs[:SPAN]
    attended_ref, query_grad_ref = refs[SPAN : SPAN + 2]
    term_refs = refs[SPAN + 2 : 2 * SPAN + 2]
    region, sums = refs[2 * SPAN + 2 :]
    cols = query_ref.shape[1]
    heads = cols // HEAD_DIM
    tiles = query_ref.shape[0] // TILE
    score_scale = 1.0 / math.sqrt(HEAD_DIM)
    slab = slab_ref[0]
    odd = (slab + group_ref[0]) & 1

    def place(n):
        return pl.ds(pl.multiple_of((n + odd * (2 * REACH - 2 * n)) * (2 * TILE), 2 * TILE), 2 * TILE)

    for n in range(SPAN):
        region[place(n), :] = tile_refs[n][...]
    sums[...] = jnp.zeros_like(sums)
    key_lows, live = [], []
    for i in range(tiles):
        for b in range(BLOCKS):
            slot = mask_ref[i, b]
            picked = align_ref[jnp.clip(slot, 0, LIST - 1), slab]
            local = jnp.clip(picked - slab + REACH, 0, SPAN - 1)
            live.append(slot >= 0)
            key_lows.append(pl.multiple_of(jnp.where(slot >= 0, local, 0) * (2 * TILE), 2 * TILE))
    units = [(i, h) for i in range(tiles) for h in range(heads)]
    state = [{} for _ in units]

    def where(u):
        i, h = units[u]
        lows = key_lows[i * BLOCKS : (i + 1) * BLOCKS]
        return pl.ds(i * TILE, TILE), pl.ds(h * HEAD_DIM, HEAD_DIM), lows, live[i * BLOCKS : (i + 1) * BLOCKS]

    def products(u):
        rows, hcols, lows, kept = where(u)
        query, grad = query_ref[rows, hcols], grad_ref[rows, hcols]
        state[u]["scores"] = [
            jnp.where(kept[b], nt(query, region[pl.ds(lows[b], TILE), hcols]) * score_scale, -jnp.inf)
            for b in range(BLOCKS)
        ]
        state[u]["grad_probs"] = [nt(grad, region[pl.ds(lows[b] + TILE, TILE), hcols]) for b in range(BLOCKS)]

    def softmax(u):
        scores = state[u].pop("scores")
        top = jnp.max(jnp.maximum(jnp.maximum(scores[0], scores[1]), scores[2]), -1, keepdims=True)
        exps = [jnp.exp(s - top) for s in scores]
        inverse = 1.0 / jnp.sum(exps[0] + exps[1] + exps[2], -1, keepdims=True)
        state[u]["probs"] = [e * inverse for e in exps]
        state[u]["weights"] = [p.astype(jnp.bfloat16) for p in state[u]["probs"]]

    def outputs(u):
        rows, hcols, lows, _ = where(u)
        weights, probs, grad_probs = (state[u][n] for n in ("weights", "probs", "grad_probs"))
        values = [region[pl.ds(low + TILE, TILE), hcols] for low in lows]
        attended = nn(weights[0], values[0]) + nn(weights[1], values[1]) + nn(weights[2], values[2])
        attended = attended.astype(jnp.bfloat16)
        attended_ref[rows, hcols] = attended
        grad = grad_ref[rows, hcols].astype(jnp.float32)
        delta = jnp.sum(grad * attended.astype(jnp.float32), -1, keepdims=True)
        state[u]["grad_scores"] = [
            (probs[b] * (grad_probs[b] - delta)).astype(jnp.bfloat16) for b in range(BLOCKS)
        ]

    def gradients(u):
        rows, hcols, lows, _ = where(u)
        weights, grad_scores = state[u]["weights"], state[u]["grad_scores"]
        query, grad = query_ref[rows, hcols], grad_ref[rows, hcols]
        keys = [region[pl.ds(low, TILE), hcols] for low in lows]
        query_grad = nn(grad_scores[0], keys[0]) + nn(grad_scores[1], keys[1]) + nn(grad_scores[2], keys[2])
        query_grad_ref[rows, hcols] = (query_grad * score_scale).astype(query_grad_ref.dtype)
        for b in range(BLOCKS):
            sums[pl.ds(lows[b], TILE), hcols] += tn(grad_scores[b], query) * score_scale
            sums[pl.ds(lows[b] + TILE, TILE), hcols] += tn(weights[b], grad)
        state[u].clear()

    stages = (products, softmax, outputs, gradients)
    for n in range(len(units) + len(stages) - 1):
        for lag, stage in tuple(enumerate(stages))[::-1]:
            if 0 <= n - lag < len(units):
                stage(n - lag)
    for n in range(SPAN):
        term_refs[n][...] = sums[place(n), :].astype(term_refs[n].dtype)


def vm():
    return pl.BlockSpec(memory_space=VMEM)


def sm():
    return pl.BlockSpec(memory_space=SMEM)


def step(queries, keys, values, out_weight, out_grad, align_lists, block_masks):
    slabs = lax.axis_size("tm")
    groups = lax.axis_size("head")
    slab = jnp.full((1,), lax.axis_index("tm"), jnp.int32)
    group = jnp.full((1,), lax.axis_index("head"), jnp.int32)
    rows, cols = queries.shape
    bf16, f32 = jnp.bfloat16, jnp.float32

    def paired(x, near):
        pairs = []
        for t in range(slabs):
            for g in range(groups):
                by = 1 if (t + g) % 2 == (0 if near else 1) else -1
                pairs.append((t * groups + g, (t + by) % slabs * groups + g))
        return lax.ppermute(x, ("tm", "head"), pairs)

    def swap(x, flip):
        return lax.ppermute(x, "head", [(g, g ^ flip) for g in range(groups)])

    def kernel(body, args, in_specs, outs, scratch=(), flops=0, limit=LIMIT, exps=0):
        moved = sum(math.prod(a.shape) * a.dtype.itemsize for a in (*args, *outs))
        return pl.pallas_call(
            body,
            out_shape=outs,
            in_specs=in_specs,
            out_specs=[vm()] * len(outs),
            scratch_shapes=list(scratch),
            compiler_params=pltpu.CompilerParams(vmem_limit_bytes=limit),
            cost_estimate=pl.CostEstimate(flops=flops, bytes_accessed=moved, transcendentals=exps),
        )(*args)

    block = jax.ShapeDtypeStruct((rows, cols), bf16)
    second = swap(out_grad, 2)
    own = jnp.stack([keys, values], 0).reshape(2 * TILE, cols)
    n1 = paired(own, True)
    m1 = paired(own, False)
    half = jnp.concatenate([out_grad, second], 0)
    other = swap(half, 6)
    m2 = paired(n1, False)
    n2 = paired(m1, True)
    mine = jnp.concatenate([lax.optimization_barrier(half), other], 0)
    theirs = swap(mine, 1)
    n3 = paired(m2, True)
    m3 = paired(n2, False)

    (grad_attended,) = kernel(
        grad_attended_kernel,
        (group, mine, theirs, out_weight),
        [sm(), vm(), vm(), vm()],
        [block],
        flops=2 * rows * cols * groups * cols,
    )
    outs = kernel(
        attention_kernel,
        (slab, group, align_lists.T, block_masks, queries, grad_attended, m3, m2, m1, own, n1, n2, n3),
        [sm()] * 4 + [vm()] * (2 + SPAN),
        [block] * (2 + REACH) + [jax.ShapeDtypeStruct(own.shape, f32)] + [block] * REACH,
        scratch=(VMEM((SPAN * 2 * TILE, cols), bf16), VMEM((SPAN * 2 * TILE, cols), f32)),
        flops=14 * rows * cols * BLOCKS * TILE,
        exps=rows * cols * BLOCKS,
    )
    attended, query_grad = outs[:2]
    terms = outs[2:]
    pair = jax.ShapeDtypeStruct((2 * rows, cols), bf16)
    send, keep_near, keep_far = kernel(
        out_proj_kernel,
        (group, attended, out_weight),
        [sm(), vm(), vm()],
        [jax.ShapeDtypeStruct((4 * rows, cols), bf16), pair, pair],
        flops=2 * rows * cols * groups * cols,
    )

    def add(x, y):
        return (x.astype(f32) + y.astype(f32)).astype(bf16)

    near3 = paired(terms[2 * REACH], True)
    far3 = paired(terms[0], False)
    far2 = paired(add(near3, terms[REACH - 2]), False)
    near2 = paired(add(far3, terms[REACH + 2]), True)
    near1 = paired(add(far2, terms[REACH + 1]), True)
    far1 = paired(add(near2, terms[REACH - 1]), False)
    swapped = swap(send, 1)
    far = swap(add(keep_far, swapped[2 * rows :]), 6)
    near = keep_near.astype(f32) + swapped[: 2 * rows].astype(f32) + far.astype(f32)
    last = swap(near[rows:].astype(bf16), 2)
    mixed = near[:rows] + last.astype(f32)
    key_grad, value_grad = (
        (terms[REACH][at] + near1[at].astype(f32) + far1[at].astype(f32)).astype(bf16)
        for at in (slice(0, TILE), slice(TILE, 2 * TILE))
    )
    return (mixed.astype(bf16), query_grad, key_grad, value_grad)


def solution(mesh):
    return jax.shard_map(
        step,
        mesh=mesh,
        in_specs=(
            P("tm", "head"),
            P("tm", "head"),
            P("tm", "head"),
            P("head", None),
            P("tm", "head"),
            P(),
            P("tm", None),
        ),
        out_specs=(P("tm", "head"), P("tm", "head"), P("tm", "head"), P("tm", "head")),
        check_vma=False,
    )
```
